256 devices in a mesh: sect: 4 (over y), pass: 16 (over z, core), qry: 4 (over x).
Axes of the slice: x: 4, y: 4, z: 8, core: 2. Of those that a mesh axis runs over, the one named last changes fastest.
Arguments:
- query_emb: bfloat16 [8192, 4096], P(('sect', 'qry')), may hold values from -0.2 to 0.2
- passage_emb: bfloat16 [16384, 4096], P(('sect', 'pass')), may hold values from -0.2 to 0.2
- block_ids: int32 [32, 64], P(('sect', 'qry')), may hold values from 0 to 255, as said below
- positives: int32 [8192], P(('sect', 'qry')), may hold values from 0 to 16383, as said below
Outputs:
- query_grad: bfloat16 [8192, 4096], P(('sect', 'qry'), 'pass')
- pool_grad: bfloat16 [16384, 4096], P(('sect', 'pass', 'qry'))
The draws below stay inside these ranges and needn't reach their ends.
Inputs may be any that keep to these rules, and one draw needn't show every extreme that they name: `block_ids`: each row names 64 different passage blocks. `positives`: the positive passage of a query lies in a block that its query block's row of block_ids names.
All inputs are finite; a program needn't handle non-finite values.
Results may differ from the reference program's by a relative error of at most 0.015.
Values may be sent and summed in bfloat16 or wider, within the bound.
A program may use at most 128 MiB of HBM per device.

```python
import jax
import jax.numpy as jnp
from jax import lax

D = 4096
QBR = 256
PBR = 64
QR_DEV = 512
PR_DEV = 256
NQ = 8192
NP = 16384
QBLK = 32
PASSAGE_BLOCKS = 256
NB = 64
N_SECT = 4
N_PASS = 16
N_QRY = 4


EMB_SCALE = 0.028


def block_pattern(key):
    base_key = jax.random.fold_in(key, 101)
    popular_seed_key, noise_key = jax.random.split(base_key)
    per_piece = PR_DEV // PBR
    block_list = jnp.arange(PASSAGE_BLOCKS, dtype=jnp.int32)
    owning_shard = block_list // per_piece % N_PASS
    popular_boost = jax.random.randint(popular_seed_key, (N_PASS,), 0, 1 << 19)
    jitter_portion = jax.random.randint(noise_key, (QBLK, PASSAGE_BLOCKS), 0, 1 << 19)
    ranking_score = (jitter_portion + popular_boost[owning_shard][None, :]) * PASSAGE_BLOCKS + block_list[None, :]
    return lax.top_k(ranking_score, NB)[1].astype(jnp.int32)


def draw_block_ids(key, part):
    return block_pattern(key)


def draw_positives(key, part):
    pattern = block_pattern(key)
    base_key = jax.random.fold_in(key, 202)
    col_key, row_key = jax.random.split(base_key)
    col_ids = jax.random.randint(col_key, (NQ,), 0, NB)
    offsets = jax.random.randint(row_key, (NQ,), 0, PBR)
    per_query = pattern[jnp.arange(NQ, dtype=jnp.int32) // QBR]
    chosen = jnp.take_along_axis(per_query, col_ids[:, None], axis=1)[:, 0]
    return (chosen * PBR + offsets).astype(jnp.int32)


def draw_passage_emb(key, part):
    base_key = jax.random.fold_in(key, 303)
    result = jax.random.truncated_normal(base_key, -6.0, 6.0, (NP, D)) * EMB_SCALE
    return result.astype(jnp.bfloat16)


def draw_query_emb(key, part):
    base_key = jax.random.fold_in(key, 404)
    result = jax.random.truncated_normal(base_key, -6.0, 6.0, (NQ, D)) * EMB_SCALE
    return result.astype(jnp.bfloat16)


def setup_inputs(seed: int = 0) -> dict:
    streams_of = jax.random.split(jax.random.key(seed), 5)
    return {
        "query_emb": draw_query_emb(jax.random.fold_in(streams_of[4], 71), 0),
        "passage_emb": draw_passage_emb(jax.random.fold_in(streams_of[4], 71), 0),
        "block_ids": draw_block_ids(jax.random.fold_in(streams_of[4], 71), 0),
        "positives": draw_positives(jax.random.fold_in(streams_of[4], 71), 0),
    }


LOGIT_SCALE = 50.0
NEG_FILL = -1e30


def reference(query_emb, passage_emb, block_ids, positives):
    embed_width = query_emb.shape[1]
    named_count = block_ids.shape[1]
    per_piece = PR_DEV // PBR
    candidates = N_SECT * PR_DEV
    pool_rows = N_PASS * candidates
    pooled = passage_emb.reshape(N_SECT, N_PASS, PR_DEV, embed_width).transpose(1, 0, 2, 3)
    pooled = pooled.reshape(pool_rows, embed_width).astype(jnp.float32)
    local_ids = jnp.arange(N_SECT * per_piece, dtype=jnp.int32)
    shard_ids = jnp.arange(N_PASS, dtype=jnp.int32)
    block_of = ((local_ids // per_piece)[None, :] * N_PASS + shard_ids[:, None]) * per_piece + (local_ids % per_piece)[None, :]
    block_of = block_of.reshape(N_PASS * N_SECT * per_piece)
    row_ids = (block_of[:, None] * PBR + jnp.arange(PBR, dtype=jnp.int32)[None, :]).reshape(pool_rows)
    group_count = N_SECT * N_QRY
    query_blocks = QR_DEV // QBR
    query_groups = query_emb.reshape(group_count, QR_DEV, embed_width)
    pattern_groups = block_ids.reshape(group_count, query_blocks, named_count)
    positive_groups = positives.reshape(group_count, QR_DEV)
    highest = lax.Precision.HIGHEST

    def one_group(pool_total, group_items):
        queries, pattern, positive = group_items
        queries_wide = queries.astype(jnp.float32)
        scores = LOGIT_SCALE * lax.dot_general(queries_wide, pooled, (((1,), (1,)), ((), ())), precision=highest)
        allowed = jnp.any(pattern[:, :, None] == block_of[None, None, :], axis=1)
        allowed_rows = jnp.broadcast_to(allowed[:, None, :, None], (query_blocks, QBR, block_of.shape[0], PBR))
        allowed_rows = allowed_rows.reshape(QR_DEV, pool_rows)
        row_top = jnp.max(jnp.where(allowed_rows, scores, NEG_FILL), axis=1, keepdims=True)
        exp_terms = jnp.where(allowed_rows, jnp.exp(scores - row_top), 0.0)
        row_sum = jnp.sum(exp_terms, axis=1, keepdims=True)
        target = (positive[:, None] == row_ids[None, :]).astype(jnp.float32)
        score_grad = (LOGIT_SCALE * (exp_terms / row_sum - target)).astype(jnp.bfloat16)
        grad_wide = lax.optimization_barrier(score_grad).astype(jnp.float32)
        shard_parts = jnp.einsum("qsc,scd->sqd", grad_wide.reshape(QR_DEV, N_PASS, candidates),
                                 pooled.reshape(N_PASS, candidates, embed_width), precision=highest)
        rounded = lax.optimization_barrier(shard_parts.astype(jnp.bfloat16)).astype(jnp.float32)
        query_grad = jnp.sum(rounded, axis=0).astype(jnp.bfloat16)
        pool_term = lax.dot_general(grad_wide, queries_wide, (((0,), (0,)), ((), ())), precision=highest)
        pool_total = pool_total + lax.optimization_barrier(pool_term.astype(jnp.bfloat16)).astype(jnp.float32)
        return pool_total, query_grad

    start_total = jnp.zeros((pool_rows, embed_width), jnp.float32)
    pool_total, query_grads = lax.scan(one_group, start_total, (query_groups, pattern_groups, positive_groups))
    query_grad = query_grads.reshape(group_count * QR_DEV, embed_width)
    pool_grad = pool_total.astype(jnp.bfloat16).reshape(N_PASS, N_SECT, PR_DEV, embed_width).transpose(1, 0, 2, 3)
    pool_grad = pool_grad.reshape(pool_rows, embed_width)
    return (query_grad, pool_grad)
```

```python
import jax
import jax.numpy as jnp
from jax import lax
from jax.experimental import pallas as pl
from jax.experimental.pallas import tpu as pltpu
from jax.sharding import PartitionSpec as P

QBR = 256
LOGIT_SCALE = 50.0
NEG_FILL = -1e30
NEG_TEST = -1e29
MESH = pl.DeviceIdType.MESH
BF = jnp.bfloat16
F32 = jnp.float32
ORDER = (0, 2, 1, 3)


def dot_nn(a, b):
    return lax.dot_general(a, b, (((1,), (0,)), ((), ())), preferred_element_type=F32)


def dot_nt(a, b):
    return lax.dot_general(a, b, (((1,), (1,)), ((), ())), preferred_element_type=F32)


def kernel(
    q_hbm, p_hbm, m_hbm, pos_hbm, qout, pout,
    qb, pb, mb, posb, sown, ssend, srecv, stat, sgt, sg, qp, pp,
    rz, rx0, rx1, fq, fps, fpr, sibs, sibr,
    loc, sib_s, sib_r, mp_s, mp_r, qy_s, qz_s, q_r, py_s, px_s, p_r,
    sx_s, sx_r, st_s, st_r, gt_s, gt_r, gg_s, gg_r,
    rz_s, rz_r, rx0_s, rx0_r, rx1_s, rx1_r, fq_s, fq_r, fp_s, fp_r, fs_s, fs_r,
):
    y = lax.axis_index("sect")
    p = lax.axis_index("pass")
    x = lax.axis_index("qry")
    z = p // 2
    c = p % 2
    o = 1 - c
    yq = y + 1 - 2 * (y % 2)
    yp = 3 - y
    zr, zl = (z + 1) % 8, (z + 7) % 8
    xr, xl = (x + 1) % 4, (x + 3) % 4
    dev_sib = (y, 2 * z + o, x)
    dev_yq = (yq, p, x)
    dev_yp = (yp, p, x)
    dev_z = ((y, 2 * zr + c, x), (y, 2 * zl + c, x))
    dev_x = ((y, p, xr), (y, p, xl))
    sends = []

    def rc(src, dst, ssem, rsem, dev):
        d = pltpu.make_async_remote_copy(
            src_ref=src, dst_ref=dst, send_sem=ssem, recv_sem=rsem, device_id=dev, device_id_type=MESH
        )
        return d

    def send(src, dst, ssem, rsem, dev):
        d = rc(src, dst, ssem, rsem, dev)
        d.start()
        sends.append(d)

    def arrived(dst, ssem, rsem, dev):
        rc(dst, dst, ssem, rsem, dev).wait_recv()

    def cols(k, core):
        return pl.ds(pl.multiple_of((2 * k + core) * 256, 256), 256)

    loads = []
    for k in range(8):
        d = pltpu.make_async_copy(p_hbm.at[:, :, cols(k, c)], pb.at[k, :, 0, c], loc.at[k])
        d.start()
        loads.append(d)
    for k in range(8):
        d = pltpu.make_async_copy(q_hbm.at[:, cols(k, c)], qb.at[k, pl.ds(0, 512)], loc.at[8 + k])
        d.start()
        loads.append(d)
    for i, (a, b) in enumerate(((m_hbm, mb), (pos_hbm, posb))):
        d = pltpu.make_async_copy(a.at[c], b.at[0], loc.at[16 + i])
        d.start()
        loads.append(d)

    barrier = pltpu.get_barrier_semaphore()

    def hello(dev):
        pl.semaphore_signal(barrier, inc=1, device_id=dev, device_id_type=MESH)

    hello(dev_sib)
    hello(dev_yp)
    hello(dev_yq)
    hello(dev_x[0])
    hello(dev_x[1])
    for j in range(1, 8):
        zz = 2 * ((z + j) % 8) + c
        hello((y, zz, x))
        hello((yq, zz, x))
    pl.semaphore_wait(barrier, 19)

    for k in range(8):
        send(p_hbm.at[:, :, cols(k, o)], pb.at[k, :, 0, c], sib_s.at[k], sib_r.at[k], dev_sib)
    for d in loads:
        d.wait()
    for i in ORDER:
        k = 2 * i + z % 2
        send(qb.at[k, pl.ds(0, 512)], qb.at[k, pl.ds(512, 512)], qy_s.at[i], q_r.at[k], dev_yq)
    for i, (a, b) in enumerate(((m_hbm, mb), (pos_hbm, posb))):
        send(a.at[c], b.at[1], mp_s.at[i], mp_r.at[i], dev_yq)
    for k in range(8):
        arrived(pb.at[k, :, 0, o], sib_s.at[k], sib_r.at[k], dev_sib)
    for i in ORDER:
        k = 2 * i + x % 2
        send(pb.at[k, :, 0], pb.at[k, :, 1], py_s.at[i], p_r.at[k], dev_yp)

    for i in ORDER:
        side = i // 2
        k = 2 * i + z % 2
        blk = qb.at[k, pl.ds(512, 512)]
        arrived(blk, qy_s.at[i], q_r.at[k], dev_yq)
        send(blk, blk, qz_s.at[i], q_r.at[k], dev_z[side])
        k = 2 * i + x % 2
        blk = pb.at[k, :, 1]
        arrived(blk, py_s.at[i], p_r.at[k], dev_yp)
        send(blk, blk, px_s.at[i], p_r.at[k], dev_x[side])
    for i in ORDER:
        side = 1 - i // 2
        k = 2 * i + (z + 1) % 2
        arrived(qb.at[k, pl.ds(512, 512)], qz_s.at[i], q_r.at[k], dev_z[side])
        k = 2 * i + (x + 1) % 2
        arrived(pb.at[k, :, 1], px_s.at[i], p_r.at[k], dev_x[side])

    def scores(blk, out):
        def tile(t, carry):
            for s in range(2):
                acc = None
                for k in range(8):
                    a = pb[k, t].reshape(256, 256)
                    b = qb[k, pl.ds(pl.multiple_of(s * 512 + blk * 256, 256), 256)]
                    d = dot_nt(a, b)
                    acc = d if acc is None else acc + d
                out[t, :, s * 256 : s * 256 + 256] = acc
            return carry

        lax.fori_loop(0, 4, tile, 0)

    scores(o, ssend)
    for t in range(4):
        send(ssend.at[t], srecv.at[t], sx_s.at[t], sx_r.at[t], dev_sib)
    scores(c, sown)
    for i, b in enumerate((mb, posb)):
        arrived(b.at[1], mp_s.at[i], mp_r.at[i], dev_yq)

    def rows_of(t):
        r = lax.broadcasted_iota(jnp.int32, (256, 256), 0)
        sec = jnp.where(r // 128 == 0, y, yp)
        blk = (sec * 16 + 2 * z + (r // 64) % 2) * 4 + t
        return blk, blk * 64 + r % 64

    tops = [jnp.full((1, 256), NEG_FILL, F32) for _ in range(2)]
    for t in range(4):
        arrived(srecv.at[t], sx_s.at[t], sx_r.at[t], dev_sib)
        blk, _ = rows_of(t)
        one_hot = (blk == lax.broadcasted_iota(jnp.int32, (256, 256), 1)).astype(BF)
        for s in range(2):
            lanes = slice(s * 256, s * 256 + 256)
            ok = dot_nn(one_hot, mb[s])
            ok = jnp.concatenate([ok, ok], axis=1) > 0.5
            v = LOGIT_SCALE * (sown[t, :, lanes] + srecv[t, :, lanes])
            v = jnp.where(ok, v, NEG_FILL)
            sown[t, :, lanes] = v
            tops[s] = jnp.maximum(tops[s], jnp.max(v, axis=0, keepdims=True))
    sums = [jnp.zeros((1, 256), F32) for _ in range(2)]
    for t in range(4):
        for s in range(2):
            v = sown[t, :, s * 256 : s * 256 + 256]
            e = jnp.where(v > NEG_TEST, jnp.exp(v - tops[s]), 0.0)
            sums[s] = sums[s] + jnp.sum(e, axis=0, keepdims=True)
    for s in range(2):
        for h in range(2):
            lanes = slice(h * 128, h * 128 + 128)
            stat[0, 2 * s + h : 2 * s + h + 1, :] = tops[s][:, lanes]
            stat[0, 4 + 2 * s + h : 5 + 2 * s + h, :] = sums[s][:, lanes]

    for j in range(8):
        zz = 2 * ((z + j) % 8) + c
        if j:
            send(stat.at[0], stat.at[j], st_s.at[j], st_r.at[j], (y, zz, x))
        send(stat.at[0], stat.at[8 + j], st_s.at[8 + j], st_r.at[8 + j], (yq, zz, x))
    for j in range(8):
        zz = 2 * ((z + 8 - j) % 8) + c
        if j:
            arrived(stat.at[j], st_s.at[j], st_r.at[j], (y, zz, x))
        arrived(stat.at[8 + j], st_s.at[8 + j], st_r.at[8 + j], (yq, zz, x))

    def part(j, row):
        if j >= 8:
            row = (row + 2) % 4 + 4 * (row // 4)
        return stat[j, row : row + 1, :]

    row_top, row_inv = [], []
    for s in range(2):
        ts, iv = [], []
        for h in range(2):
            row = 2 * s + h
            top = part(0, row)
            for j in range(1, 16):
                top = jnp.maximum(top, part(j, row))
            tot = jnp.zeros((1, 128), F32)
            for j in range(16):
                tot = tot + part(j, row + 4) * jnp.exp(part(j, row) - top)
            ts.append(top)
            iv.append(LOGIT_SCALE / tot)
        row_top.append(jnp.concatenate(ts, axis=1))
        row_inv.append(jnp.concatenate(iv, axis=1))

    for t in range(4):
        _, row = rows_of(t)
        for s in range(2):
            v = sown[t, :, s * 256 : s * 256 + 256]
            e = jnp.where(v > NEG_TEST, jnp.exp(v - row_top[s]), 0.0)
            hit = row == posb[s, 0:1, :]
            g = e * row_inv[s] - jnp.where(hit, LOGIT_SCALE, 0.0)
            at = pl.ds(pl.multiple_of(s * 512 + c * 256, 256), 256)
            sgt[t, :, at] = g.astype(BF)
            sg[s, c, :, t * 256 : t * 256 + 256] = jnp.transpose(g).astype(BF)
    for s in range(2):
        mine = sg.at[s, c]
        send(mine, mine, gg_s.at[s], gg_r.at[s], dev_sib)
    for s in range(2):
        mine = sgt.at[:, :, pl.ds(pl.multiple_of(s * 512 + c * 256, 256), 256)]
        send(mine, mine, gt_s.at[s], gt_r.at[s], dev_sib)
    for s in range(2):
        arrived(sg.at[s, o], gg_s.at[s], gg_r.at[s], dev_sib)
        theirs = sgt.at[:, :, pl.ds(pl.multiple_of(s * 512 + o * 256, 256), 256)]
        arrived(theirs, gt_s.at[s], gt_r.at[s], dev_sib)

    def dot_q(k):
        def tile(i, carry):
            s, b = i // 2, i % 2
            qp[k, s, b] = dot_nn(sg[s, b], pb[k].reshape(1024, 256)).astype(BF)
            return carry

        lax.fori_loop(0, 4, tile, 0)

    def dot_p(k):
        def tile(t, carry):
            g = dot_nn(sgt[t], qb[k])
            pp[k, t] = g.astype(BF).reshape(2, 2, 64, 256)
            return carry

        lax.fori_loop(0, 4, tile, 0)

    def plus(dst, *srcs):
        v = dst[...].astype(F32)
        for r in srcs:
            v = v + r[...].astype(F32)
        return v

    x2 = (x + 2) % 4

    def pool_first(k):
        dot_p(k)
        for side in range(2):
            send(pp.at[k, x2, side], rx0.at[side, k], rx0_s.at[side, k], rx0_r.at[side, k], dev_x[side])

    def pool_second(k):
        for side, xx in enumerate((xr, xl)):
            back = dev_x[1 - side]
            arrived(rx0.at[side, k], rx0_s.at[side, k], rx0_r.at[side, k], back)
            blk = pp.at[k, xx, side]
            blk[...] = plus(blk, rx0.at[side, k]).astype(BF)
            send(pp.at[k, xx], rx1.at[side, k], rx1_s.at[side, k], rx1_r.at[side, k], dev_x[side])

    def pool_third(k):
        for side in range(2):
            arrived(rx1.at[side, k], rx1_s.at[side, k], rx1_r.at[side, k], dev_x[1 - side])
        fps[k] = plus(pp.at[k, x, 1], rx1.at[0, k, 1], rx1.at[1, k, 1]).astype(BF)
        send(fps.at[k], fpr.at[k], fp_s.at[k], fp_r.at[k], dev_yp)

    k = (z + 4) % 8
    dot_q(k)
    for side in range(2):
        send(qp.at[k, side], rz.at[side, 0, side], rz_s.at[side, 0, side], rz_r.at[side, 0, side], dev_z[side])
    pool_first(0)
    pool_first(1)
    for h in range(1, 4):
        for side in range(2):
            k = (z + 4 - h) % 8 if side == 0 else (z + 4 + h) % 8
            dot_q(k)
            for s in range(2):
                if h > 1 or s == side:
                    came = rz.at[side, h - 1, s]
                    arrived(came, rz_s.at[side, h - 1, s], rz_r.at[side, h - 1, s], dev_z[1 - side])
                    blk = qp.at[k, s]
                    blk[...] = plus(blk, came).astype(BF)
                send(qp.at[k, s], rz.at[side, h, s], rz_s.at[side, h, s], rz_r.at[side, h, s], dev_z[side])
        pool_first(2 * h)
        pool_first(2 * h + 1)
        pool_second(2 * h - 2)
        pool_second(2 * h - 1)
    dot_q(z)
    pool_second(6)
    pool_second(7)
    for k in range(8):
        pool_third(k)
    for s in (1, 0):
        for side in range(2):
            arrived(rz.at[side, 3, s], rz_s.at[side, 3, s], rz_r.at[side, 3, s], dev_z[1 - side])
        if s == 1:
            blk = qp.at[z, 1]
            blk[...] = plus(blk, rz.at[0, 3, 1], rz.at[1, 3, 1]).astype(BF)
            send(blk, fq, fq_s, fq_r, dev_yq)

    for k in range(8):
        arrived(fpr.at[k], fp_s.at[k], fp_r.at[k], dev_yp)
        mine = plus(pp.at[k, x, 0, c], rx1.at[0, k, 0, c], rx1.at[1, k, 0, c], fpr.at[k, c])
        pout[:, cols(k, c)] = mine.astype(BF)
        sibs[k] = plus(pp.at[k, x, 0, o], rx1.at[0, k, 0, o], rx1.at[1, k, 0, o], fpr.at[k, o]).astype(BF)
    send(sibs, sibr, fs_s, fs_r, dev_sib)
    arrived(fq, fq_s, fq_r, dev_yq)
    qout[...] = plus(qp.at[z, 0], rz.at[0, 3, 0], rz.at[1, 3, 0], fq).astype(BF).reshape(512, 256)
    arrived(sibr, fs_s, fs_r, dev_sib)
    for k in range(8):
        pout[:, cols(k, o)] = sibr[k]
    for d in sends:
        d.wait_send()


def body(query_emb, passage_emb, block_ids, positives):
    names = jnp.any(block_ids[:, :, None] == jnp.arange(256, dtype=jnp.int32)[None, None, :], axis=1)
    names = jnp.broadcast_to(names[:, :, None], (2, 256, 128)).astype(BF)
    wanted = jnp.broadcast_to(positives.reshape(2, 1, QBR), (2, 8, QBR))
    anywhere = pl.BlockSpec(memory_space=pl.ANY)
    dma = pltpu.SemaphoreType.DMA
    vm = pltpu.VMEM
    return pl.pallas_call(
        kernel,
        out_shape=(jax.ShapeDtypeStruct((512, 256), BF), jax.ShapeDtypeStruct((64, 4096), BF)),
        in_specs=[anywhere] * 4,
        out_specs=[pl.BlockSpec(memory_space=pltpu.VMEM)] * 2,
        scratch_shapes=[
            vm((8, 1024, 256), BF),
            vm((8, 4, 2, 2, 64, 256), BF),
            vm((2, 256, 128), BF),
            vm((2, 8, 256), jnp.int32),
            vm((4, 256, 512), F32),
            vm((4, 256, 512), F32),
            vm((4, 256, 512), F32),
            vm((16, 8, 128), F32),
            vm((4, 256, 1024), BF),
            vm((2, 2, 256, 1024), BF),
            vm((8, 2, 2, 256, 256), BF),
            vm((8, 4, 2, 2, 64, 256), BF),
            vm((2, 4, 2, 2, 256, 256), BF),
            vm((2, 8, 2, 64, 256), BF),
            vm((2, 8, 2, 2, 64, 256), BF),
            vm((2, 256, 256), BF),
            vm((8, 2, 64, 256), BF),
            vm((8, 2, 64, 256), BF),
            vm((8, 64, 256), BF),
            vm((8, 64, 256), BF),
            dma((18,)), dma((8,)), dma((8,)), dma((2,)), dma((2,)),
            dma((4,)), dma((4,)), dma((8,)), dma((4,)), dma((4,)), dma((8,)),
            dma((4,)), dma((4,)), dma((16,)), dma((16,)), dma((2,)), dma((2,)), dma((2,)), dma((2,)),
            dma((2, 4, 2)), dma((2, 4, 2)), dma((2, 8)), dma((2, 8)), dma((2, 8)), dma((2, 8)),
            dma, dma, dma((8,)), dma((8,)), dma, dma,
        ],
        compiler_params=pltpu.CompilerParams(
            collective_id=0, has_side_effects=True, vmem_limit_bytes=60 * 1024 * 1024
        ),
    )(query_emb, passage_emb.reshape(4, 64, 4096), names, wanted)


def solution(mesh):
    return jax.shard_map(
        body,
        mesh=mesh,
        in_specs=(
            P(("sect", "qry"), None),
            P(("sect", "pass"), None),
            P(("sect", "qry"), None),
            P(("sect", "qry")),
        ),
        out_specs=(P(("sect", "qry"), "pass"), P(("sect", "pass", "qry"), None)),
        check_vma=False,
    )
```

```python
import jax
import jax.numpy as jnp
from jax import lax
from jax.experimental import pallas as pl
from jax.experimental.pallas import tpu as pltpu
from jax.sharding import PartitionSpec as P

LOGIT_SCALE = 50.0
NEG_FILL = -1e30
NEG_TEST = -1e29
MESH = pl.DeviceIdType.MESH
BF = jnp.bfloat16
F32 = jnp.float32
Q_ORDER = ((0, 0), (0, 1), (1, 0), (1, 1))
P_ORDER = ((0, 0), (1, 0), (0, 1), (1, 1))


def dot_nn(a, b):
    return lax.dot_general(a, b, (((1,), (0,)), ((), ())), preferred_element_type=F32)


def dot_nt(a, b):
    return lax.dot_general(a, b, (((1,), (1,)), ((), ())), preferred_element_type=F32)


def kernel(
    q_hbm, p_hbm, ids_hbm, pos_hbm, qout, pout,
    qb, pb, idsb, posb, sown, ssend, srecv, stat, sgt, sg, qp, pp,
    rz, rx0, rx1, fq, fps, fpr, sibs, sibr,
    loc, sib_s, sib_r, mp_s, mp_r, qy_s, qz_s, q_r, py_s, px_s, p_r,
    sx_s, sx_r, st_s, st_r, gt_s, gt_r, gg_s, gg_r,
    rz_s, rz_r, rx0_s, rx0_r, rx1_s, rx1_r, fq_s, fq_r, fp_s, fp_r, fs_s, fs_r,
):
    y = lax.axis_index("sect")
    p = lax.axis_index("pass")
    x = lax.axis_index("qry")
    z = p // 2
    c = p % 2
    o = 1 - c
    yq = y + 1 - 2 * (y % 2)
    yp = 3 - y
    zr, zl = (z + 1) % 8, (z + 7) % 8
    xr, xl = (x + 1) % 4, (x + 3) % 4
    dev_sib = (y, 2 * z + o, x)
    dev_yq = (yq, p, x)
    dev_yp = (yp, p, x)
    dev_z = ((y, 2 * zr + c, x), (y, 2 * zl + c, x))
    dev_x = ((y, p, xr), (y, p, xl))
    sends = []

    def rc(src, dst, ssem, rsem, dev):
        d = pltpu.make_async_remote_copy(
            src_ref=src, dst_ref=dst, send_sem=ssem, recv_sem=rsem, device_id=dev, device_id_type=MESH
        )
        return d

    def send(src, dst, ssem, rsem, dev):
        d = rc(src, dst, ssem, rsem, dev)
        d.start()
        sends.append(d)

    def arrived(dst, ssem, rsem, dev):
        rc(dst, dst, ssem, rsem, dev).wait_recv()

    def cols(k, core):
        return pl.ds(pl.multiple_of((2 * k + core) * 256, 256), 256)

    loads = []
    for k in range(8):
        d = pltpu.make_async_copy(p_hbm.at[:, :, cols(k, c)], pb.at[k, :, 0, c], loc.at[k])
        d.start()
        loads.append(d)
    for k in range(8):
        d = pltpu.make_async_copy(q_hbm.at[:, cols(k, c)], qb.at[k, pl.ds(0, 512)], loc.at[8 + k])
        d.start()
        loads.append(d)
    for i, (a, b) in enumerate(((ids_hbm, idsb), (pos_hbm, posb))):
        d = pltpu.make_async_copy(a, b.at[0], loc.at[16 + i])
        d.start()
        loads.append(d)

    barrier = pltpu.get_barrier_semaphore()

    def hello(dev):
        pl.semaphore_signal(barrier, inc=1, device_id=dev, device_id_type=MESH)

    hello(dev_sib)
    hello(dev_yp)
    hello(dev_yq)
    hello(dev_x[0])
    hello(dev_x[1])
    for j in range(1, 8):
        zz = 2 * ((z + j) % 8) + c
        hello((y, zz, x))
        hello((yq, zz, x))
    pl.semaphore_wait(barrier, 19)

    for k in range(8):
        send(p_hbm.at[:, :, cols(k, o)], pb.at[k, :, 0, c], sib_s.at[k], sib_r.at[k], dev_sib)
    for d in loads:
        d.wait()

    def q_unit(k, h):
        return qb.at[k, pl.ds(512 + 256 * h, 256)]

    def p_unit(k, h):
        return pb.at[k, :, 1, c if h == 0 else o]

    for u, (j, h) in enumerate(Q_ORDER):
        k = (z + 4 * j) % 8
        send(qb.at[k, pl.ds(256 * h, 256)], q_unit(k, h), qy_s.at[u], q_r.at[k, h], dev_yq)
    for u, (j, h) in enumerate(P_ORDER):
        k = (x + 4 * j) % 8
        if u == 2:
            for i in range(8):
                arrived(pb.at[i, :, 0, o], sib_s.at[i], sib_r.at[i], dev_sib)
        send(pb.at[k, :, 0, c if h == 0 else o], p_unit(k, h), py_s.at[u], p_r.at[k, h], dev_yp)
    for i, (a, b) in enumerate(((ids_hbm, idsb), (pos_hbm, posb))):
        send(a, b.at[1], mp_s.at[i], mp_r.at[i], dev_yq)

    streams = (
        (z, ((zr + 6) % 8, (zl + 2) % 8), q_unit, q_r, Q_ORDER, qy_s, qz_s, dev_yq, dev_z),
        (x, ((xr + 6) % 8, (xl + 2) % 8), p_unit, p_r, P_ORDER, py_s, px_s, dev_yp, dev_x),
    )

    def forward(st, u):
        at, passed, unit, recv, order, ysend, rsend, ydev, rdev = st
        j, h = order[u]
        k = (at + 4 * j) % 8
        arrived(unit(k, h), ysend.at[u], recv.at[k, h], ydev)
        for side in range(2):
            send(unit(k, h), unit(k, h), rsend.at[side, u], recv.at[k, h], rdev[side])

    def relay(st, h):
        at, passed, unit, recv, order, ysend, rsend, ydev, rdev = st
        for side in range(2):
            k = passed[side]
            arrived(unit(k, h), rsend.at[side, h], recv.at[k, h], rdev[1 - side])
            send(unit(k, h), unit(k, h), rsend.at[side, 4 + h], recv.at[k, h], rdev[side])

    def take(st, final):
        at, passed, unit, recv, order, ysend, rsend, ydev, rdev = st
        for k in ((at + 6) % 8, (at + 2) % 8) if final else ((passed[0] + 4) % 8, (passed[1] + 4) % 8):
            for h in range(2):
                arrived(unit(k, h), ysend.at[0], recv.at[k, h], rdev[0])

    for u in range(4):
        for st in streams:
            forward(st, u)
        if u == 1:
            for st in streams:
                relay(st, 0)
        if u == 3:
            for st in streams:
                relay(st, 1)
    for st in streams:
        take(st, False)

    def scores(blk, out, ks, more):
        def tile(t, carry):
            for s in range(2):
                acc = None
                for k in ks:
                    a = pb[k, t].reshape(256, 256)
                    b = qb[k, pl.ds(pl.multiple_of(s * 512 + blk * 256, 256), 256)]
                    d = dot_nt(a, b)
                    acc = d if acc is None else acc + d
                lanes = slice(s * 256, s * 256 + 256)
                if more:
                    acc = acc + out[t, :, lanes]
                out[t, :, lanes] = acc
            return carry

        lax.fori_loop(0, 4, tile, 0)

    late = (z + 2) % 4
    gap = ((x - z + 4) % 4 + 2) % 3 + 1
    first = (late + jnp.where(gap == 1, 2, 1)) % 4
    second = (late + jnp.where(gap == 3, 2, 3)) % 4
    gap = (late + gap) % 4
    early_ks = (first, first + 4, second, second + 4)
    late_ks = (late, late + 4, gap, gap + 4)
    scores(o, ssend, early_ks, False)
    scores(c, sown, early_ks, False)
    for st in streams:
        take(st, True)
    scores(o, ssend, late_ks, True)
    for t in range(4):
        send(ssend.at[t], srecv.at[t], sx_s.at[t], sx_r.at[t], dev_sib)
    scores(c, sown, late_ks, True)
    for i, b in enumerate((idsb, posb)):
        arrived(b.at[1], mp_s.at[i], mp_r.at[i], dev_yq)

    def rows_of(t, lanes):
        r = lax.broadcasted_iota(jnp.int32, (256, lanes), 0)
        sec = jnp.where(r // 128 == 0, y, yp)
        blk = (sec * 16 + 2 * z + (r // 64) % 2) * 4 + t
        return blk, blk * 64 + r % 64

    tops = [jnp.full((1, 256), NEG_FILL, F32) for _ in range(2)]
    for t in range(4):
        arrived(srecv.at[t], sx_s.at[t], sx_r.at[t], dev_sib)
        blk, _ = rows_of(t, 64)
        for s in range(2):
            lanes = slice(s * 256, s * 256 + 256)
            named = jnp.where(blk == idsb[s, pl.ds(c, 1), :], 1.0, 0.0)
            ok = jnp.broadcast_to(jnp.max(named, axis=1, keepdims=True), (256, 256)) > 0.5
            v = LOGIT_SCALE * (sown[t, :, lanes] + srecv[t, :, lanes])
            v = jnp.where(ok, v, NEG_FILL)
            sown[t, :, lanes] = v
            tops[s] = jnp.maximum(tops[s], jnp.max(v, axis=0, keepdims=True))
    sums = [jnp.zeros((1, 256), F32) for _ in range(2)]
    for t in range(4):
        for s in range(2):
            v = sown[t, :, s * 256 : s * 256 + 256]
            e = jnp.where(v > NEG_TEST, jnp.exp(v - tops[s]), 0.0)
            sums[s] = sums[s] + jnp.sum(e, axis=0, keepdims=True)
    for s in range(2):
        for h in range(2):
            lanes = slice(h * 128, h * 128 + 128)
            stat[0, 2 * s + h : 2 * s + h + 1, :] = tops[s][:, lanes]
            stat[0, 4 + 2 * s + h : 5 + 2 * s + h, :] = sums[s][:, lanes]

    for j in range(8):
        zz = 2 * ((z + j) % 8) + c
        if j:
            send(stat.at[0], stat.at[j], st_s.at[j], st_r.at[j], (y, zz, x))
        send(stat.at[0], stat.at[8 + j], st_s.at[8 + j], st_r.at[8 + j], (yq, zz, x))
    for j in range(8):
        zz = 2 * ((z + 8 - j) % 8) + c
        if j:
            arrived(stat.at[j], st_s.at[j], st_r.at[j], (y, zz, x))
        arrived(stat.at[8 + j], st_s.at[8 + j], st_r.at[8 + j], (yq, zz, x))

    def part(j, row):
        if j >= 8:
            row = (row + 2) % 4 + 4 * (row // 4)
        return stat[j, row : row + 1, :]

    row_top, row_inv = [], []
    for s in range(2):
        ts, iv = [], []
        for h in range(2):
            row = 2 * s + h
            top = part(0, row)
            for j in range(1, 16):
                top = jnp.maximum(top, part(j, row))
            tot = jnp.zeros((1, 128), F32)
            for j in range(16):
                tot = tot + part(j, row + 4) * jnp.exp(part(j, row) - top)
            ts.append(top)
            iv.append(LOGIT_SCALE / tot)
        row_top.append(jnp.concatenate(ts, axis=1))
        row_inv.append(jnp.concatenate(iv, axis=1))

    for t in range(4):
        _, row = rows_of(t, 256)
        for s in range(2):
            v = sown[t, :, s * 256 : s * 256 + 256]
            e = jnp.where(v > NEG_TEST, jnp.exp(v - row_top[s]), 0.0)
            want = [posb[s, pl.ds(2 * c + h, 1), :] for h in range(2)]
            hit = row == jnp.concatenate(want, axis=1)
            g = e * row_inv[s] - jnp.where(hit, LOGIT_SCALE, 0.0)
            at = pl.ds(pl.multiple_of(s * 512 + c * 256, 256), 256)
            sgt[t, :, at] = g.astype(BF)
            sg[s, c, :, t * 256 : t * 256 + 256] = jnp.transpose(g).astype(BF)
    for s in range(2):
        mine = sg.at[s, c]
        send(mine, mine, gg_s.at[s], gg_r.at[s], dev_sib)
    for s in range(2):
        mine = sgt.at[:, :, pl.ds(pl.multiple_of(s * 512 + c * 256, 256), 256)]
        send(mine, mine, gt_s.at[s], gt_r.at[s], dev_sib)
    for s in range(2):
        arrived(sg.at[s, o], gg_s.at[s], gg_r.at[s], dev_sib)
        theirs = sgt.at[:, :, pl.ds(pl.multiple_of(s * 512 + o * 256, 256), 256)]
        arrived(theirs, gt_s.at[s], gt_r.at[s], dev_sib)

    def dot_q(k):
        def tile(i, carry):
            s, b = i // 2, i % 2
            qp[k, s, b] = dot_nn(sg[s, b], pb[k].reshape(1024, 256)).astype(BF)
            return carry

        lax.fori_loop(0, 4, tile, 0)

    def dot_p(k):
        def tile(t, carry):
            g = dot_nn(sgt[t], qb[k])
            pp[k, t] = g.astype(BF).reshape(2, 2, 64, 256)
            return carry

        lax.fori_loop(0, 4, tile, 0)

    def plus(dst, *srcs):
        v = dst[...].astype(F32)
        for r in srcs:
            v = v + r[...].astype(F32)
        return v

    x2 = (x + 2) % 4

    def pool_first(k):
        dot_p(k)
        for side in range(2):
            send(pp.at[k, x2, side], rx0.at[side, k], rx0_s.at[side, k], rx0_r.at[side, k], dev_x[side])

    def pool_second(k):
        for side, xx in enumerate((xr, xl)):
            back = dev_x[1 - side]
            arrived(rx0.at[side, k], rx0_s.at[side, k], rx0_r.at[side, k], back)
            blk = pp.at[k, xx, side]
            blk[...] = plus(blk, rx0.at[side, k]).astype(BF)
            send(pp.at[k, xx], rx1.at[side, k], rx1_s.at[side, k], rx1_r.at[side, k], dev_x[side])

    def pool_third(k):
        for side in range(2):
            arrived(rx1.at[side, k], rx1_s.at[side, k], rx1_r.at[side, k], dev_x[1 - side])
        fps[k] = plus(pp.at[k, x, 1], rx1.at[0, k, 1], rx1.at[1, k, 1]).astype(BF)
        send(fps.at[k], fpr.at[k], fp_s.at[k], fp_r.at[k], dev_yp)

    k = (z + 4) % 8
    dot_q(k)
    for side in range(2):
        send(qp.at[k, side], rz.at[side, 0, side], rz_s.at[side, 0, side], rz_r.at[side, 0, side], dev_z[side])
    pool_first(0)
    pool_first(1)
    for h in range(1, 4):
        for side in range(2):
            k = (z + 4 - h) % 8 if side == 0 else (z + 4 + h) % 8
            dot_q(k)
            for s in range(2):
                if h > 1 or s == side:
                    came = rz.at[side, h - 1, s]
                    arrived(came, rz_s.at[side, h - 1, s], rz_r.at[side, h - 1, s], dev_z[1 - side])
                    blk = qp.at[k, s]
                    blk[...] = plus(blk, came).astype(BF)
                send(qp.at[k, s], rz.at[side, h, s], rz_s.at[side, h, s], rz_r.at[side, h, s], dev_z[side])
        pool_first(2 * h)
        pool_first(2 * h + 1)
        pool_second(2 * h - 2)
        pool_second(2 * h - 1)
    dot_q(z)
    pool_second(6)
    pool_second(7)
    for k in range(8):
        pool_third(k)
    for s in (1, 0):
        for side in range(2):
            arrived(rz.at[side, 3, s], rz_s.at[side, 3, s], rz_r.at[side, 3, s], dev_z[1 - side])
        if s == 1:
            blk = qp.at[z, 1]
            blk[...] = plus(blk, rz.at[0, 3, 1], rz.at[1, 3, 1]).astype(BF)
            send(blk, fq, fq_s, fq_r, dev_yq)

    for k in range(8):
        arrived(fpr.at[k], fp_s.at[k], fp_r.at[k], dev_yp)
        mine = plus(pp.at[k, x, 0, c], rx1.at[0, k, 0, c], rx1.at[1, k, 0, c], fpr.at[k, c])
        pout[:, cols(k, c)] = mine.astype(BF)
        sibs[k] = plus(pp.at[k, x, 0, o], rx1.at[0, k, 0, o], rx1.at[1, k, 0, o], fpr.at[k, o]).astype(BF)
    send(sibs, sibr, fs_s, fs_r, dev_sib)
    arrived(fq, fq_s, fq_r, dev_yq)
    qout[...] = plus(qp.at[z, 0], rz.at[0, 3, 0], rz.at[1, 3, 0], fq).astype(BF).reshape(512, 256)
    arrived(sibr, fs_s, fs_r, dev_sib)
    for k in range(8):
        pout[:, cols(k, o)] = sibr[k]
    for d in sends:
        d.wait_send()


def body(query_emb, passage_emb, block_ids, positives):
    anywhere = pl.BlockSpec(memory_space=pl.ANY)
    dma = pltpu.SemaphoreType.DMA
    vm = pltpu.VMEM
    return pl.pallas_call(
        kernel,
        out_shape=(jax.ShapeDtypeStruct((512, 256), BF), jax.ShapeDtypeStruct((64, 4096), BF)),
        in_specs=[anywhere] * 4,
        out_specs=[pl.BlockSpec(memory_space=pltpu.VMEM)] * 2,
        scratch_shapes=[
            vm((8, 1024, 256), BF),
            vm((8, 4, 2, 2, 64, 256), BF),
            vm((2, 2, 64), jnp.int32),
            vm((2, 4, 128), jnp.int32),
            vm((4, 256, 512), F32),
            vm((4, 256, 512), F32),
            vm((4, 256, 512), F32),
            vm((16, 8, 128), F32),
            vm((4, 256, 1024), BF),
            vm((2, 2, 256, 1024), BF),
            vm((8, 2, 2, 256, 256), BF),
            vm((8, 4, 2, 2, 64, 256), BF),
            vm((2, 4, 2, 2, 256, 256), BF),
            vm((2, 8, 2, 64, 256), BF),
            vm((2, 8, 2, 2, 64, 256), BF),
            vm((2, 256, 256), BF),
            vm((8, 2, 64, 256), BF),
            vm((8, 2, 64, 256), BF),
            vm((8, 64, 256), BF),
            vm((8, 64, 256), BF),
            dma((18,)), dma((8,)), dma((8,)), dma((2,)), dma((2,)),
            dma((4,)), dma((2, 6)), dma((8, 2)), dma((4,)), dma((2, 6)), dma((8, 2)),
            dma((4,)), dma((4,)), dma((16,)), dma((16,)), dma((2,)), dma((2,)), dma((2,)), dma((2,)),
            dma((2, 4, 2)), dma((2, 4, 2)), dma((2, 8)), dma((2, 8)), dma((2, 8)), dma((2, 8)),
            dma, dma, dma((8,)), dma((8,)), dma, dma,
        ],
        compiler_params=pltpu.CompilerParams(
            collective_id=0, has_side_effects=True, vmem_limit_bytes=60 * 1024 * 1024
        ),
    )(query_emb, passage_emb.reshape(4, 64, 4096), block_ids, positives.reshape(4, 128))


def solution(mesh):
    return jax.shard_map(
        body,
        mesh=mesh,
        in_specs=(
            P(("sect", "qry"), None),
            P(("sect", "pass"), None),
            P(("sect", "qry"), None),
            P(("sect", "qry")),
        ),
        out_specs=(P(("sect", "qry"), "pass"), P(("sect", "pass", "qry"), None)),
        check_vma=False,
    )
```

```python
import jax
import jax.numpy as jnp
from jax import lax
from jax.experimental import pallas as pl
from jax.experimental.pallas import tpu as pltpu
from jax.sharding import PartitionSpec as P

LOGIT_SCALE = 50.0
NEG_FILL = -1e30
NEG_TEST = -1e29
MESH = pl.DeviceIdType.MESH
BF = jnp.bfloat16
F32 = jnp.float32
Q_ORDER = ((0, 0), (0, 1), (1, 0), (1, 1))
UNITS = ((0, 0), (0, 1), (1, 1))
P_ORDER = ((0, 0), (1, 0), (0, 1), (1, 1))


def dot_nn(a, b):
    return lax.dot_general(a, b, (((1,), (0,)), ((), ())), preferred_element_type=F32)


def dot_nt(a, b):
    return lax.dot_general(a, b, (((1,), (1,)), ((), ())), preferred_element_type=F32)


def kernel(
    q_hbm, p_hbm, ids_hbm, pos_hbm, qout, pout,
    qb, pb, idsb, posb, sown, ssend, srecv, stat, sgt, sg, qp, pp,
    rz, rx0, rx1, qa, pa, fq, fps, fpr, sibs, sibr,
    loc, sib_s, sib_r, mp_s, mp_r, qy_s, qz_s, q_r, py_s, px_s, p_r,
    sx_s, sx_r, st_s, st_r, gt_s, gt_r, gg_s, gg_r,
    qa_s, qa_r, pa_s, pa_r, rz_s, rz_r, rx0_s, rx0_r, rx1_s, rx1_r, fq_s, fq_r, fp_s, fp_r, fs_s, fs_r,
):
    y = lax.axis_index("sect")
    p = lax.axis_index("pass")
    x = lax.axis_index("qry")
    z = p // 2
    c = p % 2
    o = 1 - c
    yq = y + 1 - 2 * (y % 2)
    yp = 3 - y
    zr, zl = (z + 1) % 8, (z + 7) % 8
    xr, xl = (x + 1) % 4, (x + 3) % 4
    dev_sib = (y, 2 * z + o, x)
    dev_yq = (yq, p, x)
    dev_yp = (yp, p, x)
    dev_z = ((y, 2 * zr + c, x), (y, 2 * zl + c, x))
    dev_x = ((y, p, xr), (y, p, xl))
    sends = []

    def rc(src, dst, ssem, rsem, dev):
        d = pltpu.make_async_remote_copy(
            src_ref=src, dst_ref=dst, send_sem=ssem, recv_sem=rsem, device_id=dev, device_id_type=MESH
        )
        return d

    def send(src, dst, ssem, rsem, dev):
        d = rc(src, dst, ssem, rsem, dev)
        d.start()
        sends.append(d)

    def arrived(dst, ssem, rsem, dev):
        rc(dst, dst, ssem, rsem, dev).wait_recv()

    def cols(k, core):
        return pl.ds(pl.multiple_of((2 * k + core) * 256, 256), 256)

    loads = []
    for k in range(8):
        d = pltpu.make_async_copy(p_hbm.at[:, :, cols(k, c)], pb.at[k, :, 0, c], loc.at[k])
        d.start()
        loads.append(d)
    for k in range(8):
        d = pltpu.make_async_copy(q_hbm.at[:, cols(k, c)], qb.at[k, pl.ds(0, 512)], loc.at[8 + k])
        d.start()
        loads.append(d)
    for i, (a, b) in enumerate(((ids_hbm, idsb), (pos_hbm, posb))):
        d = pltpu.make_async_copy(a, b.at[0], loc.at[16 + i])
        d.start()
        loads.append(d)

    barrier = pltpu.get_barrier_semaphore()

    def hello(dev):
        pl.semaphore_signal(barrier, inc=1, device_id=dev, device_id_type=MESH)

    hello(dev_sib)
    hello(dev_yp)
    hello(dev_yq)
    hello(dev_x[0])
    hello(dev_x[1])
    for j in range(1, 8):
        zz = 2 * ((z + j) % 8) + c
        hello((y, zz, x))
        hello((yq, zz, x))
    pl.semaphore_wait(barrier, 19)

    for k in range(8):
        send(p_hbm.at[:, :, cols(k, o)], pb.at[k, :, 0, c], sib_s.at[k], sib_r.at[k], dev_sib)
    for d in loads:
        d.wait()

    def q_unit(k, h):
        return qb.at[k, pl.ds(512 + 256 * h, 256)]

    def p_unit(k, h):
        return pb.at[k, :, 1, c if h == 0 else o]

    for u, (j, h) in enumerate(Q_ORDER):
        k = (z + 4 * j) % 8
        send(qb.at[k, pl.ds(256 * h, 256)], q_unit(k, h), qy_s.at[u], q_r.at[k, h], dev_yq)
    for u, (j, h) in enumerate(P_ORDER):
        k = (x + 4 * j) % 8
        if u == 2:
            for i in range(8):
                arrived(pb.at[i, :, 0, o], sib_s.at[i], sib_r.at[i], dev_sib)
        send(pb.at[k, :, 0, c if h == 0 else o], p_unit(k, h), py_s.at[u], p_r.at[k, h], dev_yp)
    for i, (a, b) in enumerate(((ids_hbm, idsb), (pos_hbm, posb))):
        send(a, b.at[1], mp_s.at[i], mp_r.at[i], dev_yq)

    streams = (
        (z, ((zr + 6) % 8, (zl + 2) % 8), q_unit, q_r, Q_ORDER, qy_s, qz_s, dev_yq, dev_z),
        (x, ((xr + 6) % 8, (xl + 2) % 8), p_unit, p_r, P_ORDER, py_s, px_s, dev_yp, dev_x),
    )

    def forward(st, u):
        at, passed, unit, recv, order, ysend, rsend, ydev, rdev = st
        j, h = order[u]
        k = (at + 4 * j) % 8
        arrived(unit(k, h), ysend.at[u], recv.at[k, h], ydev)
        for side in range(2):
            send(unit(k, h), unit(k, h), rsend.at[side, u], recv.at[k, h], rdev[side])

    def relay(st, h):
        at, passed, unit, recv, order, ysend, rsend, ydev, rdev = st
        for side in range(2):
            k = passed[side]
            arrived(unit(k, h), rsend.at[side, h], recv.at[k, h], rdev[1 - side])
            send(unit(k, h), unit(k, h), rsend.at[side, 4 + h], recv.at[k, h], rdev[side])

    def take(st, final):
        at, passed, unit, recv, order, ysend, rsend, ydev, rdev = st
        for k in ((at + 6) % 8, (at + 2) % 8) if final else ((passed[0] + 4) % 8, (passed[1] + 4) % 8):
            for h in range(2):
                arrived(unit(k, h), ysend.at[0], recv.at[k, h], rdev[0])

    for u in range(4):
        for st in streams:
            forward(st, u)
        if u == 1:
            for st in streams:
                relay(st, 0)
        if u == 3:
            for st in streams:
                relay(st, 1)
    for st in streams:
        take(st, False)

    def scores(blk, out, ks, more):
        def tile(t, carry):
            for s in range(2):
                acc = None
                for k in ks:
                    a = pb[k, t].reshape(256, 256)
                    b = qb[k, pl.ds(pl.multiple_of(s * 512 + blk * 256, 256), 256)]
                    d = dot_nt(a, b)
                    acc = d if acc is None else acc + d
                lanes = slice(s * 256, s * 256 + 256)
                if more:
                    acc = acc + out[t, :, lanes]
                out[t, :, lanes] = acc
            return carry

        lax.fori_loop(0, 4, tile, 0)

    late = (z + 2) % 4
    gap = ((x - z + 4) % 4 + 2) % 3 + 1
    first = (late + jnp.where(gap == 1, 2, 1)) % 4
    second = (late + jnp.where(gap == 3, 2, 3)) % 4
    gap = (late + gap) % 4
    early_ks = (first, first + 4, second, second + 4)
    late_ks = (late, late + 4, gap, gap + 4)
    scores(o, ssend, early_ks, False)
    scores(c, sown, early_ks, False)
    for st in streams:
        take(st, True)
    scores(o, ssend, late_ks, True)
    for t in range(4):
        send(ssend.at[t], srecv.at[t], sx_s.at[t], sx_r.at[t], dev_sib)
    scores(c, sown, late_ks, True)
    for i, b in enumerate((idsb, posb)):
        arrived(b.at[1], mp_s.at[i], mp_r.at[i], dev_yq)

    def rows_of(t, lanes):
        r = lax.broadcasted_iota(jnp.int32, (256, lanes), 0)
        sec = jnp.where(r // 128 == 0, y, yp)
        blk = (sec * 16 + 2 * z + (r // 64) % 2) * 4 + t
        return blk, blk * 64 + r % 64

    tops = [jnp.full((1, 256), NEG_FILL, F32) for _ in range(2)]
    for t in range(4):
        arrived(srecv.at[t], sx_s.at[t], sx_r.at[t], dev_sib)
        blk, _ = rows_of(t, 64)
        for s in range(2):
            lanes = slice(s * 256, s * 256 + 256)
            named = jnp.where(blk == idsb[s, pl.ds(c, 1), :], 1.0, 0.0)
            ok = jnp.broadcast_to(jnp.max(named, axis=1, keepdims=True), (256, 256)) > 0.5
            v = LOGIT_SCALE * (sown[t, :, lanes] + srecv[t, :, lanes])
            v = jnp.where(ok, v, NEG_FILL)
            sown[t, :, lanes] = v
            tops[s] = jnp.maximum(tops[s], jnp.max(v, axis=0, keepdims=True))
    sums = [jnp.zeros((1, 256), F32) for _ in range(2)]
    for t in range(4):
        for s in range(2):
            v = sown[t, :, s * 256 : s * 256 + 256]
            e = jnp.where(v > NEG_TEST, jnp.exp(v - tops[s]), 0.0)
            sums[s] = sums[s] + jnp.sum(e, axis=0, keepdims=True)
    for s in range(2):
        for h in range(2):
            lanes = slice(h * 128, h * 128 + 128)
            stat[0, 2 * s + h : 2 * s + h + 1, :] = tops[s][:, lanes]
            stat[0, 4 + 2 * s + h : 5 + 2 * s + h, :] = sums[s][:, lanes]

    for j in range(8):
        zz = 2 * ((z + j) % 8) + c
        if j:
            send(stat.at[0], stat.at[j], st_s.at[j], st_r.at[j], (y, zz, x))
        send(stat.at[0], stat.at[8 + j], st_s.at[8 + j], st_r.at[8 + j], (yq, zz, x))
    for j in range(8):
        zz = 2 * ((z + 8 - j) % 8) + c
        if j:
            arrived(stat.at[j], st_s.at[j], st_r.at[j], (y, zz, x))
        arrived(stat.at[8 + j], st_s.at[8 + j], st_r.at[8 + j], (yq, zz, x))

    def part(j, row):
        if j >= 8:
            row = (row + 2) % 4 + 4 * (row // 4)
        return stat[j, row : row + 1, :]

    row_top, row_inv = [], []
    for s in range(2):
        ts, iv = [], []
        for h in range(2):
            row = 2 * s + h
            top = part(0, row)
            for j in range(1, 16):
                top = jnp.maximum(top, part(j, row))
            tot = jnp.zeros((1, 128), F32)
            for j in range(16):
                tot = tot + part(j, row + 4) * jnp.exp(part(j, row) - top)
            ts.append(top)
            iv.append(LOGIT_SCALE / tot)
        row_top.append(jnp.concatenate(ts, axis=1))
        row_inv.append(jnp.concatenate(iv, axis=1))

    for t in range(4):
        _, row = rows_of(t, 256)
        for s in range(2):
            v = sown[t, :, s * 256 : s * 256 + 256]
            e = jnp.where(v > NEG_TEST, jnp.exp(v - row_top[s]), 0.0)
            want = [posb[s, pl.ds(2 * c + h, 1), :] for h in range(2)]
            hit = row == jnp.concatenate(want, axis=1)
            g = e * row_inv[s] - jnp.where(hit, LOGIT_SCALE, 0.0)
            at = pl.ds(pl.multiple_of(s * 512 + c * 256, 256), 256)
            sgt[t, :, at] = g.astype(BF)
            sg[s, c, :, t * 256 : t * 256 + 256] = jnp.transpose(g).astype(BF)
    for s in range(2):
        mine = sg.at[s, c]
        send(mine, mine, gg_s.at[s], gg_r.at[s], dev_sib)
    for s in range(2):
        mine = sgt.at[:, :, pl.ds(pl.multiple_of(s * 512 + c * 256, 256), 256)]
        send(mine, mine, gt_s.at[s], gt_r.at[s], dev_sib)
    for s in range(2):
        arrived(sg.at[s, o], gg_s.at[s], gg_r.at[s], dev_sib)

    def dot_q(k):
        def tile(i, carry):
            s, b = i // 2, i % 2
            qp[k, s, b] = dot_nn(sg[s, b], pb[k].reshape(1024, 256)).astype(BF)
            return carry

        lax.fori_loop(0, 4, tile, 0)

    def dot_p(k):
        def tile(t, carry):
            g = dot_nn(sgt[t], qb[k])
            pp[k, t] = g.astype(BF).reshape(2, 2, 64, 256)
            return carry

        lax.fori_loop(0, 4, tile, 0)

    def plus(dst, *srcs):
        v = dst[...].astype(F32)
        for r in srcs:
            v = v + r[...].astype(F32)
        return v

    def query_first(k):
        dot_q(k)
        send(qp.at[k, 1, 0], qa.at[k], qa_s.at[k], qa_r.at[k], dev_yq)

    def query_pair(k):
        arrived(qa.at[k], qa_s.at[k], qa_r.at[k], dev_yq)
        blk = qp.at[k, 0, 0]
        blk[...] = plus(blk, qa.at[k]).astype(BF)

    def ring_z(h, u):
        r, b = UNITS[u]
        for side in range(2):
            k = (z + 4 - h) % 8 if side == 0 else (z + 4 + h) % 8
            half = pl.ds(128 * side, 128)
            if h == 0:
                src, dst = qp.at[k, r, b, half], rz.at[side, 0, u, half]
            else:
                src, dst = qp.at[k, r, b], rz.at[side, h, u]
                if h == 1:
                    came, blk = rz.at[side, 0, u, half], qp.at[k, r, b, half]
                else:
                    came, blk = rz.at[side, h - 1, u], src
                arrived(came, rz_s.at[side, h - 1, u], rz_r.at[side, h - 1, u], dev_z[1 - side])
                blk[...] = plus(blk, came).astype(BF)
            send(src, dst, rz_s.at[side, h, u], rz_r.at[side, h, u], dev_z[side])

    x2 = (x + 2) % 4
    rest = pl.ds(1, 2)

    def pool_first(k):
        dot_p(k)
        send(pp.at[k, :, 1, 0], pa.at[k], pa_s.at[k], pa_r.at[k], dev_yp)
        for side in range(2):
            src = pp.at[k, x2, :, 1, pl.ds(32 * side, 32)]
            send(src, rx0.at[side, k, rest], rx0_s.at[side, k, 1], rx0_r.at[side, k, 1], dev_x[side])

    def pool_pair(k):
        arrived(pa.at[k], pa_s.at[k], pa_r.at[k], dev_yp)
        blk = pp.at[k, :, 0, 0]
        blk[...] = plus(blk, pa.at[k]).astype(BF)
        for side in range(2):
            src = pp.at[k, x2, 0, 0, pl.ds(32 * side, 32)]
            send(src, rx0.at[side, k, 0], rx0_s.at[side, k, 0], rx0_r.at[side, k, 0], dev_x[side])

    def pool_second(k, i):
        for side, xx in enumerate((xr, xl)):
            half = pl.ds(32 * side, 32)
            if i:
                src, blk, u = pp.at[k, xx, :, 1], pp.at[k, xx, :, 1, half], rest
            else:
                src, blk, u = pp.at[k, xx, 0, 0], pp.at[k, xx, 0, 0, half], 0
            came = rx0.at[side, k, u]
            arrived(came, rx0_s.at[side, k, i], rx0_r.at[side, k, i], dev_x[1 - side])
            blk[...] = plus(blk, came).astype(BF)
            send(src, rx1.at[side, k, u], rx1_s.at[side, k, i], rx1_r.at[side, k, i], dev_x[side])

    def pool_third(k):
        for side in range(2):
            arrived(rx1.at[side, k, rest], rx1_s.at[side, k, 1], rx1_r.at[side, k, 1], dev_x[1 - side])
        fps[k] = plus(pp.at[k, x, 1, 1], rx1.at[0, k, 2], rx1.at[1, k, 2]).astype(BF)
        send(fps.at[k], fpr.at[k], fp_s.at[k], fp_r.at[k], dev_yp)

    def from_z(u):
        for side in range(2):
            arrived(rz.at[side, 3, u], rz_s.at[side, 3, u], rz_r.at[side, 3, u], dev_z[1 - side])

    query_first((z + 4) % 8)
    ring_z(0, 1)
    ring_z(0, 2)
    for s in range(2):
        theirs = sgt.at[:, :, pl.ds(pl.multiple_of(s * 512 + o * 256, 256), 256)]
        arrived(theirs, gt_s.at[s], gt_r.at[s], dev_sib)
    pool_first(0)
    query_first((z + 3) % 8)
    query_first((z + 5) % 8)
    ring_z(1, 1)
    pool_first(1)
    query_pair((z + 4) % 8)
    ring_z(0, 0)
    ring_z(1, 2)
    pool_second(0, 1)
    pool_first(2)
    pool_pair(0)
    query_first((z + 2) % 8)
    query_first((z + 6) % 8)
    query_pair((z + 3) % 8)
    query_pair((z + 5) % 8)
    ring_z(1, 0)
    pool_second(1, 1)
    pool_second(0, 0)
    pool_first(3)
    pool_pair(1)
    ring_z(2, 1)
    query_first((z + 1) % 8)
    query_first((z + 7) % 8)
    pool_second(2, 1)
    pool_first(4)
    pool_second(1, 0)
    pool_pair(2)
    ring_z(2, 2)
    query_first(z)
    pool_first(5)
    pool_second(3, 1)
    pool_first(6)
    query_pair((z + 2) % 8)
    query_pair((z + 6) % 8)
    ring_z(2, 0)
    pool_second(4, 1)
    pool_first(7)
    pool_second(2, 0)
    pool_pair(3)
    pool_third(0)
    pool_third(1)
    pool_second(5, 1)
    pool_second(3, 0)
    pool_pair(4)
    ring_z(3, 2)
    pool_third(2)
    pool_third(3)
    pool_second(6, 1)
    pool_second(4, 0)
    pool_pair(5)
    query_pair((z + 1) % 8)
    query_pair((z + 7) % 8)
    ring_z(3, 1)
    pool_third(4)
    pool_second(7, 1)
    pool_second(5, 0)
    pool_pair(6)
    pool_third(5)
    ring_z(3, 0)
    pool_third(6)
    pool_second(6, 0)
    pool_pair(7)
    pool_third(7)
    query_pair(z)
    from_z(2)
    blk = qp.at[z, 1, 1]
    blk[...] = plus(blk, rz.at[0, 3, 2], rz.at[1, 3, 2]).astype(BF)
    send(blk, fq, fq_s, fq_r, dev_yq)
    pool_second(7, 0)

    for k in range(8):
        for side in range(2):
            arrived(rx1.at[side, k, 0], rx1_s.at[side, k, 0], rx1_r.at[side, k, 0], dev_x[1 - side])
        arrived(fpr.at[k], fp_s.at[k], fp_r.at[k], dev_yp)
        sibs[0, k] = plus(pp.at[k, x, 0, 0], rx1.at[0, k, 0], rx1.at[1, k, 0]).astype(BF)
        sibs[1, k] = plus(pp.at[k, x, 0, 1], rx1.at[0, k, 1], rx1.at[1, k, 1], fpr.at[k]).astype(BF)
        pout[:, cols(k, c)] = sibs[c, k]
    send(sibs.at[o], sibr, fs_s, fs_r, dev_sib)
    from_z(1)
    arrived(fq, fq_s, fq_r, dev_yq)
    qout[256:512] = plus(qp.at[z, 0, 1], rz.at[0, 3, 1], rz.at[1, 3, 1], fq).astype(BF)
    from_z(0)
    qout[0:256] = plus(qp.at[z, 0, 0], rz.at[0, 3, 0], rz.at[1, 3, 0]).astype(BF)
    arrived(sibr, fs_s, fs_r, dev_sib)
    for k in range(8):
        pout[:, cols(k, o)] = sibr[k]
    for d in sends:
        d.wait_send()


def body(query_emb, passage_emb, block_ids, positives):
    anywhere = pl.BlockSpec(memory_space=pl.ANY)
    dma = pltpu.SemaphoreType.DMA
    vm = pltpu.VMEM
    return pl.pallas_call(
        kernel,
        out_shape=(jax.ShapeDtypeStruct((512, 256), BF), jax.ShapeDtypeStruct((64, 4096), BF)),
        in_specs=[anywhere] * 4,
        out_specs=[pl.BlockSpec(memory_space=pltpu.VMEM)] * 2,
        scratch_shapes=[
            vm((8, 1024, 256), BF),
            vm((8, 4, 2, 2, 64, 256), BF),
            vm((2, 2, 64), jnp.int32),
            vm((2, 4, 128), jnp.int32),
            vm((4, 256, 512), F32),
            vm((4, 256, 512), F32),
            vm((4, 256, 512), F32),
            vm((16, 8, 128), F32),
            vm((4, 256, 1024), BF),
            vm((2, 2, 256, 1024), BF),
            vm((8, 2, 2, 256, 256), BF),
            vm((8, 4, 2, 2, 64, 256), BF),
            vm((2, 4, 3, 256, 256), BF),
            vm((2, 8, 3, 32, 256), BF),
            vm((2, 8, 3, 64, 256), BF),
            vm((8, 256, 256), BF),
            vm((8, 4, 64, 256), BF),
            vm((256, 256), BF),
            vm((8, 64, 256), BF),
            vm((8, 64, 256), BF),
            vm((2, 8, 64, 256), BF),
            vm((8, 64, 256), BF),
            dma((18,)), dma((8,)), dma((8,)), dma((2,)), dma((2,)),
            dma((4,)), dma((2, 6)), dma((8, 2)), dma((4,)), dma((2, 6)), dma((8, 2)),
            dma((4,)), dma((4,)), dma((16,)), dma((16,)), dma((2,)), dma((2,)), dma((2,)), dma((2,)),
            dma((8,)), dma((8,)), dma((8,)), dma((8,)),
            dma((2, 4, 3)), dma((2, 4, 3)), dma((2, 8, 2)), dma((2, 8, 2)), dma((2, 8, 2)), dma((2, 8, 2)),
            dma, dma, dma((8,)), dma((8,)), dma, dma,
        ],
        compiler_params=pltpu.CompilerParams(
            collective_id=0, has_side_effects=True, vmem_limit_bytes=60 * 1024 * 1024
        ),
    )(query_emb, passage_emb.reshape(4, 64, 4096), block_ids, positives.reshape(4, 128))


def solution(mesh):
    return jax.shard_map(
        body,
        mesh=mesh,
        in_specs=(
            P(("sect", "qry"), None),
            P(("sect", "pass"), None),
            P(("sect", "qry"), None),
            P(("sect", "qry")),
        ),
        out_specs=(P(("sect", "qry"), "pass"), P(("sect", "pass", "qry"), None)),
        check_vma=False,
    )
```

```python
import jax
import jax.numpy as jnp
from jax import lax
from jax.experimental import pallas as pl
from jax.experimental.pallas import tpu as pltpu
from jax.sharding import PartitionSpec as P

LOGIT_SCALE = 50.0
NEG_FILL = -1e30
NEG_TEST = -1e29
MESH = pl.DeviceIdType.MESH
BF = jnp.bfloat16
F32 = jnp.float32
Q_ORDER = ((0, 0), (0, 1), (1, 0), (1, 1))
UNITS = ((0, 0), (0, 1), (1, 1))
P_ORDER = ((0, 0), (1, 0), (0, 1), (1, 1))


def dot_nn(a, b):
    return lax.dot_general(a, b, (((1,), (0,)), ((), ())), preferred_element_type=F32)


def dot_nt(a, b):
    return lax.dot_general(a, b, (((1,), (1,)), ((), ())), preferred_element_type=F32)


def kernel(
    q_hbm, p_hbm, ids_hbm, pos_hbm, qout, pout,
    qb, pb, idsb, posb, sown, ssend, srecv, stat, sgt, sg, qp, pp,
    rz, rx0, rx1, qa, pa, fq, fps, fpr, sibs, sibr,
    loc, sib_s, sib_r, mp_s, mp_r, qy_s, qz_s, q_r, py_s, px_s, p_r,
    sx_s, sx_r, st_s, st_r, gt_s, gt_r, gg_s, gg_r,
    qa_s, qa_r, pa_s, pa_r, rz_s, rz_r, rx0_s, rx0_r, rx1_s, rx1_r, fq_s, fq_r, fp_s, fp_r, fs_s, fs_r,
):
    y = lax.axis_index("sect")
    p = lax.axis_index("pass")
    x = lax.axis_index("qry")
    z = p // 2
    c = p % 2
    o = 1 - c
    yq = y + 1 - 2 * (y % 2)
    yp = 3 - y
    zr, zl = (z + 1) % 8, (z + 7) % 8
    xr, xl = (x + 1) % 4, (x + 3) % 4
    dev_sib = (y, 2 * z + o, x)
    dev_yq = (yq, p, x)
    dev_yp = (yp, p, x)
    dev_z = ((y, 2 * zr + c, x), (y, 2 * zl + c, x))
    dev_x = ((y, p, xr), (y, p, xl))
    sends = []

    def rc(src, dst, ssem, rsem, dev):
        d = pltpu.make_async_remote_copy(
            src_ref=src, dst_ref=dst, send_sem=ssem, recv_sem=rsem, device_id=dev, device_id_type=MESH
        )
        return d

    def send(src, dst, ssem, rsem, dev):
        d = rc(src, dst, ssem, rsem, dev)
        d.start()
        sends.append(d)

    def arrived(dst, ssem, rsem, dev):
        rc(dst, dst, ssem, rsem, dev).wait_recv()

    def cols(k, core):
        return pl.ds(pl.multiple_of((2 * k + core) * 256, 256), 256)

    loads = []
    for k in range(8):
        d = pltpu.make_async_copy(p_hbm.at[:, :, cols(k, c)], pb.at[k, :, 0, c], loc.at[k])
        d.start()
        loads.append(d)
    for k in range(8):
        d = pltpu.make_async_copy(q_hbm.at[:, cols(k, c)], qb.at[k, pl.ds(0, 512)], loc.at[8 + k])
        d.start()
        loads.append(d)
    for i, (a, b) in enumerate(((ids_hbm, idsb), (pos_hbm, posb))):
        d = pltpu.make_async_copy(a, b.at[0], loc.at[16 + i])
        d.start()
        loads.append(d)

    barrier = pltpu.get_barrier_semaphore()

    def hello(dev):
        pl.semaphore_signal(barrier, inc=1, device_id=dev, device_id_type=MESH)

    hello(dev_sib)
    hello(dev_yp)
    hello(dev_yq)
    hello(dev_x[0])
    hello(dev_x[1])
    for j in range(1, 8):
        zz = 2 * ((z + j) % 8) + c
        hello((y, zz, x))
        hello((yq, zz, x))
    pl.semaphore_wait(barrier, 19)

    for k in range(8):
        send(p_hbm.at[:, :, cols(k, o)], pb.at[k, :, 0, c], sib_s.at[k], sib_r.at[k], dev_sib)
    for d in loads:
        d.wait()

    def q_unit(k, h):
        return qb.at[k, pl.ds(512 + 256 * h, 256)]

    def p_unit(k, h):
        return pb.at[k, :, 1, c if h == 0 else o]

    for u, (j, h) in enumerate(Q_ORDER):
        k = (z + 4 * j) % 8
        send(qb.at[k, pl.ds(256 * h, 256)], q_unit(k, h), qy_s.at[u], q_r.at[k, h], dev_yq)
    for u, (j, h) in enumerate(P_ORDER):
        k = (x + 4 * j) % 8
        if u == 2:
            for i in range(8):
                arrived(pb.at[i, :, 0, o], sib_s.at[i], sib_r.at[i], dev_sib)
        send(pb.at[k, :, 0, c if h == 0 else o], p_unit(k, h), py_s.at[u], p_r.at[k, h], dev_yp)
    for i, (a, b) in enumerate(((ids_hbm, idsb), (pos_hbm, posb))):
        send(a, b.at[1], mp_s.at[i], mp_r.at[i], dev_yq)

    streams = (
        (z, ((zr + 6) % 8, (zl + 2) % 8), q_unit, q_r, Q_ORDER, qy_s, qz_s, dev_yq, dev_z),
        (x, ((xr + 6) % 8, (xl + 2) % 8), p_unit, p_r, P_ORDER, py_s, px_s, dev_yp, dev_x),
    )

    def forward(st, u):
        at, passed, unit, recv, order, ysend, rsend, ydev, rdev = st
        j, h = order[u]
        k = (at + 4 * j) % 8
        arrived(unit(k, h), ysend.at[u], recv.at[k, h], ydev)
        for side in range(2):
            send(unit(k, h), unit(k, h), rsend.at[side, u], recv.at[k, h], rdev[side])

    def relay(st, h):
        at, passed, unit, recv, order, ysend, rsend, ydev, rdev = st
        for side in range(2):
            k = passed[side]
            arrived(unit(k, h), rsend.at[side, h], recv.at[k, h], rdev[1 - side])
            send(unit(k, h), unit(k, h), rsend.at[side, 4 + h], recv.at[k, h], rdev[side])

    def take(st, final):
        at, passed, unit, recv, order, ysend, rsend, ydev, rdev = st
        for k in ((at + 6) % 8, (at + 2) % 8) if final else ((passed[0] + 4) % 8, (passed[1] + 4) % 8):
            for h in range(2):
                arrived(unit(k, h), ysend.at[0], recv.at[k, h], rdev[0])

    for u in range(4):
        for st in streams:
            forward(st, u)
        if u == 1:
            for st in streams:
                relay(st, 0)
        if u == 3:
            for st in streams:
                relay(st, 1)
    for st in streams:
        take(st, False)

    def scores(blk, out, ks, more):
        def tile(t, carry):
            for s in range(2):
                acc = None
                for k in ks:
                    a = pb[k, t].reshape(256, 256)
                    b = qb[k, pl.ds(pl.multiple_of(s * 512 + blk * 256, 256), 256)]
                    d = dot_nt(a, b)
                    acc = d if acc is None else acc + d
                lanes = slice(s * 256, s * 256 + 256)
                if more:
                    acc = acc + out[t, :, lanes]
                out[t, :, lanes] = acc
            return carry

        lax.fori_loop(0, 4, tile, 0)

    late = (z + 2) % 4
    gap = ((x - z + 4) % 4 + 2) % 3 + 1
    first = (late + jnp.where(gap == 1, 2, 1)) % 4
    second = (late + jnp.where(gap == 3, 2, 3)) % 4
    gap = (late + gap) % 4
    early_ks = (first, first + 4, second, second + 4)
    late_ks = (late, late + 4, gap, gap + 4)
    scores(o, ssend, early_ks, False)
    scores(c, sown, early_ks, False)
    for st in streams:
        take(st, True)
    scores(o, ssend, late_ks, True)
    for t in range(4):
        send(ssend.at[t], srecv.at[t], sx_s.at[t], sx_r.at[t], dev_sib)
    scores(c, sown, late_ks, True)
    for i, b in enumerate((idsb, posb)):
        arrived(b.at[1], mp_s.at[i], mp_r.at[i], dev_yq)

    def rows_of(t, lanes):
        r = lax.broadcasted_iota(jnp.int32, (256, lanes), 0)
        sec = jnp.where(r // 128 == 0, y, yp)
        blk = (sec * 16 + 2 * z + (r // 64) % 2) * 4 + t
        return blk, blk * 64 + r % 64

    tops = [jnp.full((1, 256), NEG_FILL, F32) for _ in range(2)]
    for t in range(4):
        arrived(srecv.at[t], sx_s.at[t], sx_r.at[t], dev_sib)
        blk, _ = rows_of(t, 64)
        for s in range(2):
            lanes = slice(s * 256, s * 256 + 256)
            named = jnp.where(blk == idsb[s, pl.ds(c, 1), :], 1.0, 0.0)
            ok = jnp.broadcast_to(jnp.max(named, axis=1, keepdims=True), (256, 256)) > 0.5
            v = LOGIT_SCALE * (sown[t, :, lanes] + srecv[t, :, lanes])
            v = jnp.where(ok, v, NEG_FILL)
            sown[t, :, lanes] = v
            tops[s] = jnp.maximum(tops[s], jnp.max(v, axis=0, keepdims=True))
    sums = [jnp.zeros((1, 256), F32) for _ in range(2)]
    for t in range(4):
        for s in range(2):
            v = sown[t, :, s * 256 : s * 256 + 256]
            e = jnp.where(v > NEG_TEST, jnp.exp(v - tops[s]), 0.0)
            sums[s] = sums[s] + jnp.sum(e, axis=0, keepdims=True)
    for s in range(2):
        for h in range(2):
            lanes = slice(h * 128, h * 128 + 128)
            stat[0, 2 * s + h : 2 * s + h + 1, :] = tops[s][:, lanes]
            stat[0, 4 + 2 * s + h : 5 + 2 * s + h, :] = sums[s][:, lanes]

    for j in range(8):
        zz = 2 * ((z + j) % 8) + c
        if j:
            send(stat.at[0], stat.at[j], st_s.at[j], st_r.at[j], (y, zz, x))
        send(stat.at[0], stat.at[8 + j], st_s.at[8 + j], st_r.at[8 + j], (yq, zz, x))
    for j in range(8):
        zz = 2 * ((z + 8 - j) % 8) + c
        if j:
            arrived(stat.at[j], st_s.at[j], st_r.at[j], (y, zz, x))
        arrived(stat.at[8 + j], st_s.at[8 + j], st_r.at[8 + j], (yq, zz, x))

    def part(j, row):
        if j >= 8:
            row = (row + 2) % 4 + 4 * (row // 4)
        return stat[j, row : row + 1, :]

    row_top, row_inv = [], []
    for s in range(2):
        ts, iv = [], []
        for h in range(2):
            row = 2 * s + h
            top = part(0, row)
            for j in range(1, 16):
                top = jnp.maximum(top, part(j, row))
            tot = jnp.zeros((1, 128), F32)
            for j in range(16):
                tot = tot + part(j, row + 4) * jnp.exp(part(j, row) - top)
            ts.append(top)
            iv.append(LOGIT_SCALE / tot)
        row_top.append(jnp.concatenate(ts, axis=1))
        row_inv.append(jnp.concatenate(iv, axis=1))

    for s in range(2):
        want = [posb[s, pl.ds(2 * c + h, 1), :] for h in range(2)]
        want = jnp.concatenate(want, axis=1)
        at = pl.ds(pl.multiple_of(s * 512 + c * 256, 256), 256)
        for t in range(4):
            _, row = rows_of(t, 256)
            v = sown[t, :, s * 256 : s * 256 + 256]
            e = jnp.where(v > NEG_TEST, jnp.exp(v - row_top[s]), 0.0)
            g = e * row_inv[s] - jnp.where(row == want, LOGIT_SCALE, 0.0)
            sgt[t, :, at] = g.astype(BF)
            sg[s, c, :, t * 256 : t * 256 + 256] = jnp.transpose(g).astype(BF)
        mine = sg.at[s, c]
        send(mine, mine, gg_s.at[s], gg_r.at[s], dev_sib)
    for s in range(2):
        mine = sgt.at[:, :, pl.ds(pl.multiple_of(s * 512 + c * 256, 256), 256)]
        send(mine, mine, gt_s.at[s], gt_r.at[s], dev_sib)
    for s in range(2):
        arrived(sg.at[s, o], gg_s.at[s], gg_r.at[s], dev_sib)

    def dot_q(k):
        def tile(i, carry):
            s, b = i // 2, i % 2
            qp[k, s, b] = dot_nn(sg[s, b], pb[k].reshape(1024, 256)).astype(BF)
            return carry

        lax.fori_loop(0, 4, tile, 0)

    def dot_p(k):
        def tile(t, carry):
            g = dot_nn(sgt[t], qb[k])
            pp[k, t] = g.astype(BF).reshape(2, 2, 64, 256)
            return carry

        lax.fori_loop(0, 4, tile, 0)

    def plus(dst, *srcs):
        v = dst[...].astype(F32)
        for r in srcs:
            v = v + r[...].astype(F32)
        return v

    def query_first(k):
        dot_q(k)
        send(qp.at[k, 1, 0], qa.at[k], qa_s.at[k], qa_r.at[k], dev_yq)

    def query_pair(k):
        arrived(qa.at[k], qa_s.at[k], qa_r.at[k], dev_yq)
        blk = qp.at[k, 0, 0]
        blk[...] = plus(blk, qa.at[k]).astype(BF)

    def ring_z(h, u):
        r, b = UNITS[u]
        for side in range(2):
            k = (z + 4 - h) % 8 if side == 0 else (z + 4 + h) % 8
            half = pl.ds(128 * side, 128)
            if h == 0:
                src, dst = qp.at[k, r, b, half], rz.at[side, 0, u, half]
            else:
                src, dst = qp.at[k, r, b], rz.at[side, h, u]
                if h == 1:
                    came, blk = rz.at[side, 0, u, half], qp.at[k, r, b, half]
                else:
                    came, blk = rz.at[side, h - 1, u], src
                arrived(came, rz_s.at[side, h - 1, u], rz_r.at[side, h - 1, u], dev_z[1 - side])
                blk[...] = plus(blk, came).astype(BF)
            send(src, dst, rz_s.at[side, h, u], rz_r.at[side, h, u], dev_z[side])

    x2 = (x + 2) % 4
    rest = pl.ds(1, 2)

    def pool_first(k):
        dot_p(k)
        send(pp.at[k, :, 1, 0], pa.at[k], pa_s.at[k], pa_r.at[k], dev_yp)
        for side in range(2):
            src = pp.at[k, x2, :, 1, pl.ds(32 * side, 32)]
            send(src, rx0.at[side, k, rest], rx0_s.at[side, k, 1], rx0_r.at[side, k, 1], dev_x[side])

    def pool_pair(k):
        arrived(pa.at[k], pa_s.at[k], pa_r.at[k], dev_yp)
        blk = pp.at[k, :, 0, 0]
        blk[...] = plus(blk, pa.at[k]).astype(BF)
        for side in range(2):
            src = pp.at[k, x2, 0, 0, pl.ds(32 * side, 32)]
            send(src, rx0.at[side, k, 0], rx0_s.at[side, k, 0], rx0_r.at[side, k, 0], dev_x[side])

    def pool_second(k, i):
        for side, xx in enumerate((xr, xl)):
            half = pl.ds(32 * side, 32)
            if i:
                src, blk, u = pp.at[k, xx, :, 1], pp.at[k, xx, :, 1, half], rest
            else:
                src, blk, u = pp.at[k, xx, 0, 0], pp.at[k, xx, 0, 0, half], 0
            came = rx0.at[side, k, u]
            arrived(came, rx0_s.at[side, k, i], rx0_r.at[side, k, i], dev_x[1 - side])
            blk[...] = plus(blk, came).astype(BF)
            send(src, rx1.at[side, k, u], rx1_s.at[side, k, i], rx1_r.at[side, k, i], dev_x[side])

    def pool_third(k):
        for side in range(2):
            arrived(rx1.at[side, k, rest], rx1_s.at[side, k, 1], rx1_r.at[side, k, 1], dev_x[1 - side])
        fps[k] = plus(pp.at[k, x, 1, 1], rx1.at[0, k, 2], rx1.at[1, k, 2]).astype(BF)
        send(fps.at[k], fpr.at[k], fp_s.at[k], fp_r.at[k], dev_yp)

    def from_z(u):
        for side in range(2):
            arrived(rz.at[side, 3, u], rz_s.at[side, 3, u], rz_r.at[side, 3, u], dev_z[1 - side])

    query_first((z + 4) % 8)
    ring_z(0, 1)
    ring_z(0, 2)
    for s in range(2):
        theirs = sgt.at[:, :, pl.ds(pl.multiple_of(s * 512 + o * 256, 256), 256)]
        arrived(theirs, gt_s.at[s], gt_r.at[s], dev_sib)
    pool_first(0)
    query_first((z + 3) % 8)
    query_first((z + 5) % 8)
    ring_z(1, 1)
    pool_first(1)
    query_pair((z + 4) % 8)
    ring_z(0, 0)
    ring_z(1, 2)
    pool_second(0, 1)
    pool_first(2)
    pool_pair(0)
    query_first((z + 2) % 8)
    query_first((z + 6) % 8)
    query_pair((z + 3) % 8)
    query_pair((z + 5) % 8)
    ring_z(1, 0)
    pool_second(1, 1)
    pool_second(0, 0)
    pool_first(3)
    pool_pair(1)
    ring_z(2, 1)
    query_first((z + 1) % 8)
    query_first((z + 7) % 8)
    pool_second(2, 1)
    pool_first(4)
    pool_second(1, 0)
    pool_pair(2)
    ring_z(2, 2)
    query_first(z)
    pool_first(5)
    pool_second(3, 1)
    pool_first(6)
    query_pair((z + 2) % 8)
    query_pair((z + 6) % 8)
    ring_z(2, 0)
    pool_second(4, 1)
    pool_first(7)
    pool_second(2, 0)
    pool_pair(3)
    pool_third(0)
    pool_third(1)
    pool_second(5, 1)
    pool_second(3, 0)
    pool_pair(4)
    ring_z(3, 2)
    pool_third(2)
    pool_third(3)
    pool_second(6, 1)
    pool_second(4, 0)
    pool_pair(5)
    query_pair((z + 1) % 8)
    query_pair((z + 7) % 8)
    ring_z(3, 1)
    pool_third(4)
    pool_second(7, 1)
    pool_second(5, 0)
    pool_pair(6)
    pool_third(5)
    ring_z(3, 0)
    pool_third(6)
    pool_second(6, 0)
    pool_pair(7)
    pool_third(7)
    query_pair(z)
    from_z(2)
    blk = qp.at[z, 1, 1]
    blk[...] = plus(blk, rz.at[0, 3, 2], rz.at[1, 3, 2]).astype(BF)
    send(blk, fq, fq_s, fq_r, dev_yq)
    pool_second(7, 0)

    for k in range(8):
        for side in range(2):
            arrived(rx1.at[side, k, 0], rx1_s.at[side, k, 0], rx1_r.at[side, k, 0], dev_x[1 - side])
        arrived(fpr.at[k], fp_s.at[k], fp_r.at[k], dev_yp)
        sibs[0, k] = plus(pp.at[k, x, 0, 0], rx1.at[0, k, 0], rx1.at[1, k, 0]).astype(BF)
        sibs[1, k] = plus(pp.at[k, x, 0, 1], rx1.at[0, k, 1], rx1.at[1, k, 1], fpr.at[k]).astype(BF)
        pout[:, cols(k, c)] = sibs[c, k]
    send(sibs.at[o], sibr, fs_s, fs_r, dev_sib)
    from_z(1)
    arrived(fq, fq_s, fq_r, dev_yq)
    qout[256:512] = plus(qp.at[z, 0, 1], rz.at[0, 3, 1], rz.at[1, 3, 1], fq).astype(BF)
    from_z(0)
    qout[0:256] = plus(qp.at[z, 0, 0], rz.at[0, 3, 0], rz.at[1, 3, 0]).astype(BF)
    arrived(sibr, fs_s, fs_r, dev_sib)
    for k in range(8):
        pout[:, cols(k, o)] = sibr[k]
    for d in sends:
        d.wait_send()


def body(query_emb, passage_emb, block_ids, positives):
    anywhere = pl.BlockSpec(memory_space=pl.ANY)
    dma = pltpu.SemaphoreType.DMA
    vm = pltpu.VMEM
    return pl.pallas_call(
        kernel,
        out_shape=(jax.ShapeDtypeStruct((512, 256), BF), jax.ShapeDtypeStruct((64, 4096), BF)),
        in_specs=[anywhere] * 4,
        out_specs=[pl.BlockSpec(memory_space=pltpu.VMEM)] * 2,
        scratch_shapes=[
            vm((8, 1024, 256), BF),
            vm((8, 4, 2, 2, 64, 256), BF),
            vm((2, 2, 64), jnp.int32),
            vm((2, 4, 128), jnp.int32),
            vm((4, 256, 512), F32),
            vm((4, 256, 512), F32),
            vm((4, 256, 512), F32),
            vm((16, 8, 128), F32),
            vm((4, 256, 1024), BF),
            vm((2, 2, 256, 1024), BF),
            vm((8, 2, 2, 256, 256), BF),
            vm((8, 4, 2, 2, 64, 256), BF),
            vm((2, 4, 3, 256, 256), BF),
            vm((2, 8, 3, 32, 256), BF),
            vm((2, 8, 3, 64, 256), BF),
            vm((8, 256, 256), BF),
            vm((8, 4, 64, 256), BF),
            vm((256, 256), BF),
            vm((8, 64, 256), BF),
            vm((8, 64, 256), BF),
            vm((2, 8, 64, 256), BF),
            vm((8, 64, 256), BF),
            dma((18,)), dma((8,)), dma((8,)), dma((2,)), dma((2,)),
            dma((4,)), dma((2, 6)), dma((8, 2)), dma((4,)), dma((2, 6)), dma((8, 2)),
            dma((4,)), dma((4,)), dma((16,)), dma((16,)), dma((2,)), dma((2,)), dma((2,)), dma((2,)),
            dma((8,)), dma((8,)), dma((8,)), dma((8,)),
            dma((2, 4, 3)), dma((2, 4, 3)), dma((2, 8, 2)), dma((2, 8, 2)), dma((2, 8, 2)), dma((2, 8, 2)),
            dma, dma, dma((8,)), dma((8,)), dma, dma,
        ],
        compiler_params=pltpu.CompilerParams(
            collective_id=0, has_side_effects=True, vmem_limit_bytes=60 * 1024 * 1024
        ),
    )(query_emb, passage_emb.reshape(4, 64, 4096), block_ids, positives.reshape(4, 128))


def solution(mesh):
    return jax.shard_map(
        body,
        mesh=mesh,
        in_specs=(
            P(("sect", "qry"), None),
            P(("sect", "pass"), None),
            P(("sect", "qry"), None),
            P(("sect", "qry")),
        ),
        out_specs=(P(("sect", "qry"), "pass"), P(("sect", "pass", "qry"), None)),
        check_vma=False,
    )
```
